128 devices in a mesh: ctx: 4 (over y), heads: 32 (over x, z, core).
Axes of the slice: x: 4, y: 4, z: 4, core: 2. Of those that a mesh axis runs over, the one named last changes fastest.
Arguments:
- queries: float32 [32768, 4096], P(('ctx', 'heads')), may hold values from -110 to 110
- keys: float32 [32768, 4096], P(('ctx', 'heads')), may hold values from -4 to 4
- values: float32 [32768, 4096], P(('ctx', 'heads')), may hold values from -12 to 12
- merge_keys: float32 [6, 256, 512], replicated, may hold values from -0.25 to 0.25
- merge_values: float32 [6, 256, 512], replicated, may hold values from -0.25 to 0.25
- out_gain: float32 [32, 128], P('heads'), may hold values from 0.1 to 1.9
Outputs:
- attended: float32 [32768, 4096], P(('ctx', 'heads'))
The draws below stay inside these ranges and needn't reach their ends.
All inputs are finite; a program needn't handle non-finite values.
Results may differ from the reference program's by a relative error of at most 0.0003.
Values sent between devices are 32-bit elements; how exact they have to be, the bound alone decides.
A program may use at most 256 MiB of HBM per device.

```python
import math
import jax
import jax.numpy as jnp
from jax import lax

HD = 128
LEAF = 256
HEADS = 32
TOKENS = 32768
LEAVES = 128
LEVELS = 7


def query_key_pair(key):
    full_width = HEADS * HD
    query_seed = jax.random.fold_in(key, 101)
    key_seed = jax.random.fold_in(key, 202)
    key_rows = jnp.clip(jax.random.normal(key_seed, (TOKENS, full_width), jnp.float32), -4.0, 4.0)
    query_rows = 1.5 * jnp.clip(jax.random.normal(query_seed, (TOKENS, full_width), jnp.float32), -4.0, 4.0)
    return (query_rows, key_rows)


def draw_queries(key, part):
    return query_key_pair(key)[0]


def draw_keys(key, part):
    return query_key_pair(key)[1]


def draw_values(key, part):
    full_width = HEADS * HD
    scale_seed = jax.random.fold_in(key, 404)
    noise_seed = jax.random.fold_in(key, 505)
    row_scale = jnp.exp(jax.random.uniform(scale_seed, (TOKENS, 1), jnp.float32, math.log(0.3), math.log(3.0)))
    noise_part = jnp.clip(jax.random.normal(noise_seed, (TOKENS, full_width), jnp.float32), -4.0, 4.0)
    return row_scale * noise_part


def centred(stream_key, dims, width, bound, dtype=jnp.bfloat16):
    result = jax.random.normal(stream_key, dims, jnp.float32) * width
    return jnp.minimum(jnp.maximum(result, -bound), bound).astype(dtype)


def setup_inputs(seed: int = 0) -> dict:
    streams_of = jax.random.split(jax.random.key(seed), 7)
    return {
        "queries": draw_queries(jax.random.fold_in(streams_of[6], 71), 0),
        "keys": draw_keys(jax.random.fold_in(streams_of[6], 71), 0),
        "values": draw_values(jax.random.fold_in(streams_of[6], 71), 0),
        "merge_keys": centred(streams_of[3], (LEVELS - 1, LEAF, 2 * LEAF), (2 * LEAF) ** -0.5, 0.25, jnp.float32),
        "merge_values": centred(streams_of[4], (LEVELS - 1, LEAF, 2 * LEAF), (2 * LEAF) ** -0.5, 0.25, jnp.float32),
        "out_gain": jnp.clip(1.0 + 0.18 * jax.random.normal(streams_of[5], (HEADS, HD), jnp.float32), 0.1, 1.9),
    }


def merge_nodes(matrix, children):
    node_count = children.shape[0] // 2
    paired = children.reshape(node_count, 2 * children.shape[1], children.shape[2])
    return jnp.einsum('ij,njw->niw', matrix, paired, precision=lax.Precision.HIGHEST)

def sibling_nodes(key_nodes):
    node_count, row_count, feature_width = key_nodes.shape
    return key_nodes.reshape(node_count // 2, 2, row_count, feature_width)[:, ::-1].reshape(node_count, row_count, feature_width)

def split_heads(matrix):
    return matrix.reshape(TOKENS, HEADS, HD).transpose(1, 0, 2)

def reference(queries, keys, values, merge_keys, merge_values, out_gain):
    score_scale = 1.0 / math.sqrt(HD)

    def one_head(inputs):
        head_queries, head_keys, head_values, head_gain = inputs
        key_nodes = head_keys.reshape(LEAVES, LEAF, HD)
        value_nodes = head_values.reshape(LEAVES, LEAF, HD)
        key_parts = [key_nodes]
        value_parts = [value_nodes]
        for level_index in range(LEVELS):
            key_parts.append(jnp.repeat(sibling_nodes(key_nodes), 2 ** level_index, axis=0))
            value_parts.append(jnp.repeat(sibling_nodes(value_nodes), 2 ** level_index, axis=0))
            if level_index + 1 < LEVELS:
                key_nodes = merge_nodes(merge_keys[level_index], key_nodes)
                value_nodes = merge_nodes(merge_values[level_index], value_nodes)
        all_keys = jnp.concatenate(key_parts, axis=1)
        all_values = jnp.concatenate(value_parts, axis=1)
        grouped = head_queries.reshape(LEAVES, LEAF, HD)
        scores = jnp.einsum('nqd,nkd->nqk', grouped, all_keys, precision=lax.Precision.HIGHEST) * score_scale
        weights = jax.nn.softmax(scores, axis=-1)
        context = jnp.einsum('nqk,nkd->nqd', weights, all_values, precision=lax.Precision.HIGHEST).reshape(TOKENS, HD)
        mean_square = lax.optimization_barrier(jnp.mean(context * context, axis=-1, keepdims=True))
        return context * lax.rsqrt(mean_square + 1e-06) * head_gain
    outputs = lax.map(one_head, (split_heads(queries), split_heads(keys), split_heads(values), out_gain))
    return outputs.transpose(1, 0, 2).reshape(TOKENS, HEADS * HD)
```

```python
import functools
import math

import jax
import jax.numpy as jnp
from jax import lax
from jax.experimental import pallas as pl
from jax.experimental.pallas import tpu as pltpu
from jax.sharding import PartitionSpec as P

MESH = pl.DeviceIdType.MESH
F32, BF16 = jnp.float32, jnp.bfloat16
SLOTS = 2
OUT_SLOTS = 2
AHEAD = 3


def tree_levels(ctx, heads):
    z_size = min(4, heads // 2)
    digits = [
        ("heads", 1, 2),
        ("heads", 2, z_size),
        ("heads", 2 * z_size, heads // (2 * z_size)),
        ("ctx", 1, ctx),
    ]
    return [
        (axis, stride, size, bit)
        for axis, stride, size in digits
        for bit in range(size.bit_length() - 1)
    ]


def split(x):
    hi = x.astype(BF16)
    return hi, (x - hi.astype(F32)).astype(BF16)


def halves(x):
    return jnp.concatenate(split(x), axis=1)


def dot(a, b):
    return jnp.dot(a, b, preferred_element_type=F32)


def dot_nt(a, b):
    return lax.dot_general(a, b, (((1,), (1,)), ((), ())), preferred_element_type=F32)


def kernel(
    levels, q, k, v, merge_k, merge_v, gain, out,
    qb, xb, rb, sb, mw, stage, kc, vc, ob, gb,
    load_sem, lend_sem, borrow_sem, send_sem, recv_sem,
    put_sem, give_sem, take_sem, mat_sem, gain_sem, gain_send, gain_recv,
):
    count, rows, width = qb.shape[0], qb.shape[1] // 2, qb.shape[2]
    merges = len(levels) - 1
    here = {axis: lax.axis_index(axis) for axis in ("ctx", "heads")}
    mine = here["heads"]
    core = mine % 2
    args = (k, v, q)
    landing = (xb.at[0], xb.at[1], qb)

    def digit(level):
        axis, stride, size, _ = levels[level]
        return here[axis] // stride % size

    def side(level):
        return digit(level) // 2 ** levels[level][3] % 2

    def partner(level):
        axis, stride, size, bit = levels[level]
        d = digit(level)
        other = size - 1 - d if bit else d + 1 - 2 * (d % 2)
        return {axis: here[axis] + stride * (other - d)}

    partners = [partner(level) for level in range(len(levels))]

    def columns(owner, head):
        return pl.ds(pl.multiple_of((owner * count + head) * width, width), width)

    def leaf(owner):
        return pl.ds(pl.multiple_of(owner * rows, rows), rows)

    def load(i, head):
        return pltpu.make_async_copy(
            args[i].at[:, columns(core, head)],
            landing[i].at[head, leaf(core)],
            load_sem.at[i, head],
        )

    def lend(i, head):
        return pltpu.make_async_remote_copy(
            src_ref=args[i].at[:, columns(1 - core, head)],
            dst_ref=landing[i].at[head, leaf(core)],
            send_sem=lend_sem.at[i, head],
            recv_sem=borrow_sem.at[i, head],
            device_id=partners[0],
            device_id_type=MESH,
        )

    def borrow(i, head):
        return pltpu.make_async_remote_copy(
            src_ref=args[i].at[:, columns(core, head)],
            dst_ref=landing[i].at[head, leaf(1 - core)],
            send_sem=lend_sem.at[i, head],
            recv_sem=borrow_sem.at[i, head],
            device_id=partners[0],
            device_id_type=MESH,
        )

    def pass_on(level, i, head):
        return pltpu.make_async_remote_copy(
            src_ref=sb.at[level, i, head % SLOTS],
            dst_ref=rb.at[level, i, head],
            send_sem=send_sem.at[level, i, head % SLOTS],
            recv_sem=recv_sem.at[level, i, head],
            device_id=partners[level + 1],
            device_id_type=MESH,
        )

    def put(head):
        return pltpu.make_async_copy(
            ob.at[head % OUT_SLOTS, leaf(core)],
            out.at[:, columns(core, head)],
            put_sem.at[head % OUT_SLOTS],
        )

    def give(head):
        return pltpu.make_async_remote_copy(
            src_ref=ob.at[head % OUT_SLOTS, leaf(1 - core)],
            dst_ref=out.at[:, columns(core, head)],
            send_sem=give_sem.at[head % OUT_SLOTS],
            recv_sem=take_sem.at[head],
            device_id=partners[0],
            device_id_type=MESH,
        )

    def take(head):
        return pltpu.make_async_remote_copy(
            src_ref=ob.at[head % OUT_SLOTS, leaf(1 - core)],
            dst_ref=out.at[:, columns(1 - core, head)],
            send_sem=give_sem.at[head % OUT_SLOTS],
            recv_sem=take_sem.at[head],
            device_id=partners[0],
            device_id_type=MESH,
        )

    def matrix(level, i):
        return pltpu.make_async_copy(
            (merge_k, merge_v)[i].at[level], stage.at[2 * level + i], mat_sem.at[level, i]
        )

    gain_levels = [n for n, level in enumerate(levels) if level[0] == "heads"]

    def swap_gain(n, sender):
        span = 2**n
        start = sender // span * span
        return pltpu.make_async_remote_copy(
            src_ref=gb.at[pl.ds(start, span)],
            dst_ref=gb.at[pl.ds(start, span)],
            send_sem=gain_send.at[n],
            recv_sem=gain_recv.at[n],
            device_id=partners[n],
            device_id_type=MESH,
        )

    def gain_step(n):
        if n > 0:
            swap_gain(n - 1, mine).wait_send()
            swap_gain(n - 1, partners[n - 1]["heads"]).wait_recv()
        if n < len(gain_levels):
            swap_gain(n, mine).start()

    own_gain = pltpu.make_async_copy(gain, gb.at[mine], gain_sem)
    own_gain.start()
    for level in range(merges):
        for i in range(2):
            matrix(level, i).start()
    barrier = pltpu.get_barrier_semaphore()
    for other in partners:
        pl.semaphore_signal(barrier, inc=1, device_id=other, device_id_type=MESH)
    pl.semaphore_wait(barrier, len(partners))

    def fetch(i, head):
        lend(i, head).start()
        load(i, head).start()

    for head in range(min(AHEAD, count)):
        fetch(0, head)
        fetch(1, head)
    own_gain.wait()
    for level in range(merges):
        for i in range(2):
            matrix(level, i).wait()
            hi, lo = split(stage[2 * level + i])
            mw[level, i, 0, :rows] = hi[:, :rows]
            mw[level, i, 0, rows:] = lo[:, :rows]
            mw[level, i, 1, :rows] = hi[:, rows:]
            mw[level, i, 1, rows:] = lo[:, rows:]

    def ready(level, i, head):
        if level == 0:
            load(i, head).wait()
            borrow(i, head).wait_recv()
        else:
            pass_on(level - 1, i, head).wait_recv()

        @pl.when(head >= SLOTS)
        def _():
            pass_on(level, i, head - SLOTS).wait_send()

    def merge(level, i, head):
        if level == 0:
            lower, upper = xb[i, head, :rows], xb[i, head, rows:]
            first, second = 0, 1
        else:
            lower, upper = sb[level - 1, i, head % SLOTS], rb[level - 1, i, head]
            first = side(level)
            second = 1 - first
        both = dot(mw[level, i, first], halves(lower)) + dot(mw[level, i, second], halves(upper))
        summed = both[:rows] + both[rows:]
        sb[level, i, head % SLOTS] = summed[:, :width] + summed[:, width:]

    def advance(t, i, guarded):
        if guarded:
            for level in range(merges):
                head = t - level

                @pl.when((head >= 0) & (head < count))
                def _(level=level, head=head):
                    ready(level, i, head)
                    merge(level, i, head)

            for level in range(merges):
                head = t - level

                @pl.when((head >= 0) & (head < count))
                def _(level=level, head=head):
                    pass_on(level, i, head).start()
        else:
            for level in range(merges):
                ready(level, i, t - level)
            for level in range(merges):
                merge(level, i, t - level)
            for level in range(merges):
                pass_on(level, i, t - level).start()

    def attend(head):
        for i in range(2):
            pass_on(merges - 1, i, head).wait_recv()
        for i in range(3):
            lend(i, head).wait_send()
        load(2, head).wait()
        borrow(2, head).wait_recv()
        for cat, i in ((kc, 0), (vc, 1)):
            for n in range(merges + 2):
                block = xb[i, head, n * rows : (n + 1) * rows] if n < 2 else rb[n - 2, i, head]
                cat[n * rows : (n + 1) * rows] = halves(block)

        @pl.when(head >= OUT_SLOTS)
        def _():
            put(head - OUT_SLOTS).wait()
            give(head - OUT_SLOTS).wait_send()

        scale = math.log2(math.e) / math.sqrt(width)
        scale_out = gb[core * count + head]
        hi, lo = kc[:, :width], kc[:, width:]
        keys = jnp.concatenate([hi, hi, lo, lo], axis=1)
        for part in range(2):
            span = slice(part * rows, (part + 1) * rows)
            query = halves(qb[head, span] * scale)
            scores = dot_nt(jnp.concatenate([query, query], axis=1), keys)
            top = jnp.max(scores, axis=1, keepdims=True)
            weights = jnp.exp2(scores - top)
            total = jnp.sum(weights, axis=1, keepdims=True)
            high, low = split(weights)
            both = dot(high, vc[...]) + dot(low, vc[...])
            context = (both[:, :width] + both[:, width:]) / total
            mean_square = jnp.mean(context * context, axis=1, keepdims=True)
            ob[head % OUT_SLOTS, span] = context * lax.rsqrt(mean_square + 1e-06) * scale_out
        put(head).start()
        give(head).start()

    def request(t):
        @pl.when(t + AHEAD < count)
        def _():
            fetch(0, t + AHEAD)
            fetch(1, t + AHEAD)

        @pl.when((t >= AHEAD) & (t - AHEAD < count))
        def _():
            fetch(2, t - AHEAD)

    @pl.loop(0, merges)
    def _(t):
        for n in range(len(gain_levels) + 1):

            @pl.when(t == n)
            def _(n=n):
                gain_step(n)

        request(t)
        advance(t, 0, True)
        advance(t, 1, True)

    @pl.loop(merges, count)
    def _(t):
        request(t)
        advance(t, 0, False)
        advance(t, 1, False)
        attend(t - merges)

    @pl.loop(max(merges, count), count + merges)
    def _(t):
        request(t)
        advance(t, 0, True)
        advance(t, 1, True)
        attend(t - merges)

    for head in range(count - SLOTS, count):
        for level in range(merges):
            for i in range(2):
                pass_on(level, i, head).wait_send()
    for head in range(count - OUT_SLOTS, count):
        put(head).wait()
        give(head).wait_send()

    @pl.loop(0, count)
    def _(head):
        take(head).wait_recv()


def solution(mesh):
    levels = tree_levels(mesh.shape["ctx"], mesh.shape["heads"])
    merges = len(levels) - 1

    def shards(queries, keys, values, merge_keys, merge_values, out_gain):
        rows, columns = queries.shape
        width = out_gain.shape[1]
        heads = columns // width
        count = heads // 2
        gain_steps = sum(level[0] == "heads" for level in levels)
        dma = pltpu.SemaphoreType.DMA
        return pl.pallas_call(
            functools.partial(kernel, levels),
            out_shape=jax.ShapeDtypeStruct((rows, columns), F32),
            in_specs=[pl.BlockSpec(memory_space=pl.ANY)] * 6,
            out_specs=pl.BlockSpec(memory_space=pl.ANY),
            scratch_shapes=[
                pltpu.VMEM((count, 2 * rows, width), F32),
                pltpu.VMEM((2, count, 2 * rows, width), F32),
                pltpu.VMEM((merges, 2, count, rows, width), F32),
                pltpu.VMEM((merges, 2, SLOTS, rows, width), F32),
                pltpu.VMEM((merges, 2, 2, 2 * rows, rows), BF16),
                pltpu.VMEM((2 * merges, rows, 2 * rows), F32),
                pltpu.VMEM(((merges + 2) * rows, 2 * width), BF16),
                pltpu.VMEM(((merges + 2) * rows, 2 * width), BF16),
                pltpu.VMEM((OUT_SLOTS, 2 * rows, width), F32),
                pltpu.VMEM((heads, 1, width), F32),
                dma((3, count)),
                dma((3, count)),
                dma((3, count)),
                dma((merges, 2, SLOTS)),
                dma((merges, 2, count)),
                dma((OUT_SLOTS,)),
                dma((OUT_SLOTS,)),
                dma((count,)),
                dma((merges, 2)),
                dma,
                dma((gain_steps,)),
                dma((gain_steps,)),
            ],
            compiler_params=pltpu.CompilerParams(
                collective_id=0, has_side_effects=True, vmem_limit_bytes=67043328
            ),
            name="multipole",
        )(queries, keys, values, merge_keys, merge_values, out_gain)

    return jax.shard_map(
        shards,
        mesh=mesh,
        in_specs=(
            P(("ctx", "heads"), None),
            P(("ctx", "heads"), None),
            P(("ctx", "heads"), None),
            P(),
            P(),
            P("heads", None),
        ),
        out_specs=P(("ctx", "heads"), None),
        check_vma=False,
    )
```

```python
import functools
import math

import jax
import jax.numpy as jnp
from jax import lax
from jax.experimental import pallas as pl
from jax.experimental.pallas import tpu as pltpu
from jax.sharding import PartitionSpec as P

MESH = pl.DeviceIdType.MESH
F32, BF16 = jnp.float32, jnp.bfloat16
SLOTS = 2
OUT_SLOTS = 2
AHEAD = 3
CHUNK = 16
STEP = 3
BEHIND = 2


def tree_levels(ctx, heads):
    z_size = min(4, heads // 2)
    digits = [
        ("heads", 1, 2),
        ("heads", 2, z_size),
        ("heads", 2 * z_size, heads // (2 * z_size)),
        ("ctx", 1, ctx),
    ]
    return [
        (axis, stride, size, bit)
        for axis, stride, size in digits
        for bit in range(size.bit_length() - 1)
    ]


def split(x):
    hi = x.astype(BF16)
    return hi, (x - hi.astype(F32)).astype(BF16)


def halves(x):
    return jnp.concatenate(split(x), axis=1)


def dot(a, b):
    return jnp.dot(a, b, preferred_element_type=F32)


def dot_nt(a, b):
    return lax.dot_general(a, b, (((1,), (1,)), ((), ())), preferred_element_type=F32)


def kernel(
    levels, q, k, v, merge_k, merge_v, gain, out,
    qb, xb, rb, sb, mw, stage, kc, vc, wb, tb, ob, gb,
    load_sem, lend_sem, borrow_sem, send_sem, recv_sem,
    put_sem, give_sem, take_sem, mat_sem, gain_sem, gain_send, gain_recv,
):
    count, rows, width = qb.shape[0], qb.shape[1] // 2, qb.shape[2]
    merges = len(levels) - 1
    here = {axis: lax.axis_index(axis) for axis in ("ctx", "heads")}
    mine = here["heads"]
    core = mine % 2
    args = (k, v, q)
    landing = (xb.at[0], xb.at[1], qb)

    def digit(level):
        axis, stride, size, _ = levels[level]
        return here[axis] // stride % size

    def side(level):
        return digit(level) // 2 ** levels[level][3] % 2

    def partner(level):
        axis, stride, size, bit = levels[level]
        d = digit(level)
        other = size - 1 - d if bit else d + 1 - 2 * (d % 2)
        return {axis: here[axis] + stride * (other - d)}

    def sides(level):
        return side(level) if isinstance(level, int) else 0

    partners = [partner(level) for level in range(len(levels))]

    def columns(owner, head):
        return pl.ds(pl.multiple_of((owner * count + head) * width, width), width)

    def leaf(owner):
        return pl.ds(pl.multiple_of(owner * rows, rows), rows)

    def load(i, head):
        return pltpu.make_async_copy(
            args[i].at[:, columns(core, head)],
            landing[i].at[head, leaf(core)],
            load_sem.at[i, head],
        )

    def lend(i, head):
        return pltpu.make_async_remote_copy(
            src_ref=args[i].at[:, columns(1 - core, head)],
            dst_ref=landing[i].at[head, leaf(core)],
            send_sem=lend_sem.at[i, head],
            recv_sem=borrow_sem.at[i, head],
            device_id=partners[0],
            device_id_type=MESH,
        )

    def borrow(i, head):
        return pltpu.make_async_remote_copy(
            src_ref=args[i].at[:, columns(core, head)],
            dst_ref=landing[i].at[head, leaf(1 - core)],
            send_sem=lend_sem.at[i, head],
            recv_sem=borrow_sem.at[i, head],
            device_id=partners[0],
            device_id_type=MESH,
        )

    def pass_on(level, i, head):
        return pltpu.make_async_remote_copy(
            src_ref=sb.at[level, i, head % SLOTS],
            dst_ref=rb.at[level, i, head],
            send_sem=send_sem.at[level, i, head % SLOTS],
            recv_sem=recv_sem.at[level, i, head],
            device_id=partners[level + 1],
            device_id_type=MESH,
        )

    def put(head):
        return pltpu.make_async_copy(
            ob.at[head % OUT_SLOTS, leaf(core)],
            out.at[:, columns(core, head)],
            put_sem.at[head % OUT_SLOTS],
        )

    def give(head):
        return pltpu.make_async_remote_copy(
            src_ref=ob.at[head % OUT_SLOTS, leaf(1 - core)],
            dst_ref=out.at[:, columns(core, head)],
            send_sem=give_sem.at[head % OUT_SLOTS],
            recv_sem=take_sem.at[head],
            device_id=partners[0],
            device_id_type=MESH,
        )

    def take(head):
        return pltpu.make_async_remote_copy(
            src_ref=ob.at[head % OUT_SLOTS, leaf(1 - core)],
            dst_ref=out.at[:, columns(1 - core, head)],
            send_sem=give_sem.at[head % OUT_SLOTS],
            recv_sem=take_sem.at[head],
            device_id=partners[0],
            device_id_type=MESH,
        )

    def matrix(level, i, which):
        at = which
        if not (isinstance(level, int) and level == 0):
            at = lax.rem(which + sides(level), 2)
        return pltpu.make_async_copy(
            (merge_k, merge_v)[i].at[level, :, pl.ds(pl.multiple_of(at * rows, rows), rows)],
            stage.at[2 * level + i, :, pl.ds(which * rows, rows)],
            mat_sem.at[level, i, which],
        )

    gain_levels = [n for n, level in enumerate(levels) if level[0] == "heads"]

    def swap_gain(n, sender):
        span = 2**n
        start = sender // span * span
        return pltpu.make_async_remote_copy(
            src_ref=gb.at[pl.ds(start, span)],
            dst_ref=gb.at[pl.ds(start, span)],
            send_sem=gain_send.at[n],
            recv_sem=gain_recv.at[n],
            device_id=partners[n],
            device_id_type=MESH,
        )

    def gain_step(n):
        if n > 0:
            swap_gain(n - 1, mine).wait_send()
            swap_gain(n - 1, partners[n - 1]["heads"]).wait_recv()
        if n < len(gain_levels):
            swap_gain(n, mine).start()

    own_gain = pltpu.make_async_copy(gain, gb.at[mine], gain_sem)
    own_gain.start()
    for level in range(merges):
        for i in range(2):
            for which in range(2):
                matrix(level, i, which).start()
    barrier = pltpu.get_barrier_semaphore()
    for other in partners:
        pl.semaphore_signal(barrier, inc=1, device_id=other, device_id_type=MESH)
    pl.semaphore_wait(barrier, len(partners))

    def fetch(i, head):
        lend(i, head).start()
        load(i, head).start()

    for head in range(min(AHEAD, count)):
        fetch(0, head)
        fetch(1, head)
    own_gain.wait()

    def unpack(level):
        for i in range(2):
            for which in range(2):
                matrix(level, i, which).wait()
            hi, lo = split(stage[2 * level + i])
            mw[level, i, :rows] = hi
            mw[level, i, rows:] = lo

    unpack(0)

    def ready(level, i, head):
        if level == 0:
            load(i, head).wait()
            borrow(i, head).wait_recv()
        else:
            pass_on(level - 1, i, head).wait_recv()

        @pl.when(head >= SLOTS)
        def _():
            pass_on(level, i, head - SLOTS).wait_send()

    def merge(level, i, head):
        if level == 0:
            first, second = xb[i, head, :rows], xb[i, head, rows:]
        else:
            first, second = sb[level - 1, i, head % SLOTS], rb[level - 1, i, head]
        pair = jnp.concatenate([halves(first), halves(second)], axis=0)
        both = dot(mw[level, i], pair)
        summed = both[:rows] + both[rows:]
        sb[level, i, head % SLOTS] = summed[:, :width] + summed[:, width:]

    def when(level, i):
        return STEP * level + i * BEHIND

    def nodes(t, third):
        return [
            (level, i, t - (when(level, i) - third) // 3)
            for i in range(2)
            for level in reversed(range(merges))
            if (when(level, i) - third) % 3 == 0
        ]

    def advance(t, third, guarded):
        todo = nodes(t, third)
        if guarded:
            for level, i, head in todo:

                @pl.when((head >= 0) & (head < count))
                def _(level=level, i=i, head=head):
                    ready(level, i, head)
                    merge(level, i, head)

            for level, i, head in todo:

                @pl.when((head >= 0) & (head < count))
                def _(level=level, i=i, head=head):
                    pass_on(level, i, head).start()
        else:
            for node in todo:
                ready(*node)
            for node in todo:
                merge(*node)
            for node in todo:
                pass_on(*node).start()

    blocks = merges + 2
    spans = blocks * rows // stage.shape[2]

    def gather(cat, i, head, n):
        block = xb[i, head, n * rows : (n + 1) * rows] if n < 2 else rb[n - 2, i, head]
        cat[n * rows : (n + 1) * rows] = halves(block)

    def gathers(cat, i, head):
        return [functools.partial(gather, cat, i, head, n) for n in range(blocks)]

    def score(head, part):
        each = stage.shape[2]
        span = slice(part * rows, (part + 1) * rows)
        query = halves(qb[head, span] * (math.log2(math.e) / math.sqrt(width)))
        query = jnp.concatenate([query, query], axis=1)
        hi, lo = kc[:, :width], kc[:, width:]
        block = dot_nt(query, jnp.concatenate([hi, hi, lo, lo], axis=1))
        for n in range(spans):
            stage[part * spans + n] = block[:, n * each : (n + 1) * each]

    def soften(part, row):
        scores = jnp.concatenate(
            [stage[part * spans + n, row : row + CHUNK] for n in range(spans)], axis=1
        )
        top = jnp.max(scores, axis=1, keepdims=True)
        weights = jnp.exp2(scores - top)
        hi, lo = split(weights)
        at = part * rows + row
        tb[at : at + CHUNK] = jnp.sum(weights, axis=1, keepdims=True)
        wb[at : at + CHUNK] = hi
        wb[2 * rows + at : 2 * rows + at + CHUNK] = lo

    def softens(part):
        return [functools.partial(soften, part, row) for row in range(0, rows, CHUNK)]

    def collect(head):
        for i in range(3):
            lend(i, head).wait_send()

        @pl.when(head >= OUT_SLOTS)
        def _():
            put(head - OUT_SLOTS).wait()
            give(head - OUT_SLOTS).wait_send()

        for part in range(2):
            span = slice(part * rows, (part + 1) * rows)
            low = slice((part + 2) * rows, (part + 3) * rows)
            both = dot(wb[span], vc[...]) + dot(wb[low], vc[...])
            context = (both[:, :width] + both[:, width:]) / tb[span]
            mean_square = jnp.mean(context * context, axis=1, keepdims=True)
            normed = context * lax.rsqrt(mean_square + 1e-06)
            ob[head % OUT_SLOTS, span] = normed * gb[core * count + head]

    lag = -(-max(when(merges - 1, 0) + 3, when(merges - 1, 1) + 1) // 3)

    def request(t):
        @pl.when(t + AHEAD < count)
        def _():
            fetch(0, t + AHEAD)
            fetch(1, t + AHEAD)

        @pl.when((t >= lag - 2) & (t - lag + 2 < count))
        def _():
            fetch(2, t - lag + 2)

    @pl.loop(0, lag)
    def _(t):
        request(t)
        for third in range(3):
            if third < 2:
                for n in range(len(gain_levels) + 1):
                    if n % 2 == third:

                        @pl.when(t == n // 2)
                        def _(n=n):
                            gain_step(n)

            advance(t, third, True)
            for level in range(1, merges):
                before = when(level, 0) - 2
                if before % 3 == third:

                    @pl.when(t == before // 3)
                    def _(level=level):
                        unpack(level)

    def whole(t, guarded):
        head = t - lag
        request(t)
        advance(t, 0, guarded)
        pass_on(merges - 1, 0, head).wait_recv()
        load(2, head).wait()
        borrow(2, head).wait_recv()
        for task in gathers(kc, 0, head):
            task()
        score(head, 0)
        advance(t, 1, guarded)
        score(head, 1)
        for task in softens(0):
            task()
        advance(t, 2, guarded)
        pass_on(merges - 1, 1, head).wait_recv()
        for task in gathers(vc, 1, head) + softens(1):
            task()
        collect(head)
        put(head).start()
        give(head).start()

    @pl.loop(lag, count)
    def _(t):
        whole(t, False)

    @pl.loop(max(lag, count), count + lag)
    def _(t):
        whole(t, True)

    for head in range(count - SLOTS, count):
        for level in range(merges):
            for i in range(2):
                pass_on(level, i, head).wait_send()
    for head in range(count - OUT_SLOTS, count):
        put(head).wait()
        give(head).wait_send()

    @pl.loop(0, count)
    def _(head):
        take(head).wait_recv()


def solution(mesh):
    levels = tree_levels(mesh.shape["ctx"], mesh.shape["heads"])
    merges = len(levels) - 1

    def shards(queries, keys, values, merge_keys, merge_values, out_gain):
        rows, columns = queries.shape
        width = out_gain.shape[1]
        heads = columns // width
        count = heads // 2
        gain_steps = sum(level[0] == "heads" for level in levels)
        dma = pltpu.SemaphoreType.DMA
        return pl.pallas_call(
            functools.partial(kernel, levels),
            out_shape=jax.ShapeDtypeStruct((rows, columns), F32),
            in_specs=[pl.BlockSpec(memory_space=pl.ANY)] * 6,
            out_specs=pl.BlockSpec(memory_space=pl.ANY),
            scratch_shapes=[
                pltpu.VMEM((count, 2 * rows, width), F32),
                pltpu.VMEM((2, count, 2 * rows, width), F32),
                pltpu.VMEM((merges, 2, count, rows, width), F32),
                pltpu.VMEM((merges, 2, SLOTS, rows, width), F32),
                pltpu.VMEM((merges, 2, 2 * rows, 2 * rows), BF16),
                pltpu.VMEM((2 * merges, rows, 2 * rows), F32),
                pltpu.VMEM(((merges + 2) * rows, 2 * width), BF16),
                pltpu.VMEM(((merges + 2) * rows, 2 * width), BF16),
                pltpu.VMEM((4 * rows, (merges + 2) * rows), BF16),
                pltpu.VMEM((2 * rows, 1), F32),
                pltpu.VMEM((OUT_SLOTS, 2 * rows, width), F32),
                pltpu.VMEM((heads, 1, width), F32),
                dma((3, count)),
                dma((3, count)),
                dma((3, count)),
                dma((merges, 2, SLOTS)),
                dma((merges, 2, count)),
                dma((OUT_SLOTS,)),
                dma((OUT_SLOTS,)),
                dma((count,)),
                dma((merges, 2, 2)),
                dma,
                dma((gain_steps,)),
                dma((gain_steps,)),
            ],
            compiler_params=pltpu.CompilerParams(
                collective_id=0, has_side_effects=True, vmem_limit_bytes=67043328
            ),
            name="multipole",
        )(queries, keys, values, merge_keys, merge_values, out_gain)

    return jax.shard_map(
        shards,
        mesh=mesh,
        in_specs=(
            P(("ctx", "heads"), None),
            P(("ctx", "heads"), None),
            P(("ctx", "heads"), None),
            P(),
            P(),
            P("heads", None),
        ),
        out_specs=P(("ctx", "heads"), None),
        check_vma=False,
    )
```

```python
import functools
import math

import jax
import jax.numpy as jnp
from jax import lax
from jax.experimental import pallas as pl
from jax.experimental.pallas import tpu as pltpu
from jax.sharding import PartitionSpec as P

MESH = pl.DeviceIdType.MESH
F32, BF16 = jnp.float32, jnp.bfloat16
SLOTS = 2
OUT_SLOTS = 2
AHEAD = 3
CHUNK = 16
STEP = 3
BEHIND = 2
GROUPS = 1


def tree_levels(ctx, heads):
    z_size = min(4, heads // 2)
    digits = [
        ("heads", 1, 2),
        ("heads", 2, z_size),
        ("heads", 2 * z_size, heads // (2 * z_size)),
        ("ctx", 1, ctx),
    ]
    return [
        (axis, stride, size, bit)
        for axis, stride, size in digits
        for bit in range(size.bit_length() - 1)
    ]


def split(x):
    hi = x.astype(BF16)
    return hi, (x - hi.astype(F32)).astype(BF16)


def halves(x):
    return jnp.concatenate(split(x), axis=1)


def dot(a, b):
    return jnp.dot(a, b, preferred_element_type=F32)


def dot_nt(a, b):
    return lax.dot_general(a, b, (((1,), (1,)), ((), ())), preferred_element_type=F32)


def kernel(
    levels, q, k, v, merge_k, merge_v, gain, out,
    qb, xb, rb, sb, mw, stage, kc, vc, wb, tb, ob, gb,
    load_sem, lend_sem, borrow_sem, send_sem, recv_sem,
    put_sem, give_sem, take_sem, mat_sem, gain_sem, gain_send, gain_recv,
):
    count, rows, width = qb.shape[0], qb.shape[1] // 2, qb.shape[2]
    merges = len(levels) - 1
    here = {axis: lax.axis_index(axis) for axis in ("ctx", "heads")}
    mine = here["heads"]
    core = mine % 2
    args = (k, v, q)
    landing = (xb.at[0], xb.at[1], qb)

    def digit(level):
        axis, stride, size, _ = levels[level]
        return here[axis] // stride % size

    def side(level):
        return digit(level) // 2 ** levels[level][3] % 2

    def partner(level):
        axis, stride, size, bit = levels[level]
        d = digit(level)
        other = size - 1 - d if bit else d + 1 - 2 * (d % 2)
        return {axis: here[axis] + stride * (other - d)}

    def sides(level):
        return side(level) if isinstance(level, int) else 0

    partners = [partner(level) for level in range(len(levels))]

    def columns(owner, head):
        return pl.ds(pl.multiple_of((owner * count + head) * width, width), width)

    def leaf(owner):
        return pl.ds(pl.multiple_of(owner * rows, rows), rows)

    def load(i, head):
        return pltpu.make_async_copy(
            args[i].at[:, columns(core, head)],
            landing[i].at[head, leaf(core)],
            load_sem.at[i, head],
        )

    def lend(i, head):
        return pltpu.make_async_remote_copy(
            src_ref=args[i].at[:, columns(1 - core, head)],
            dst_ref=landing[i].at[head, leaf(core)],
            send_sem=lend_sem.at[i, head],
            recv_sem=borrow_sem.at[i, head],
            device_id=partners[0],
            device_id_type=MESH,
        )

    def borrow(i, head):
        return pltpu.make_async_remote_copy(
            src_ref=args[i].at[:, columns(core, head)],
            dst_ref=landing[i].at[head, leaf(1 - core)],
            send_sem=lend_sem.at[i, head],
            recv_sem=borrow_sem.at[i, head],
            device_id=partners[0],
            device_id_type=MESH,
        )

    def pass_on(level, i, head):
        return pltpu.make_async_remote_copy(
            src_ref=sb.at[level, i, head % SLOTS],
            dst_ref=rb.at[level, i, head],
            send_sem=send_sem.at[level, i, head % SLOTS],
            recv_sem=recv_sem.at[level, i, head],
            device_id=partners[level + 1],
            device_id_type=MESH,
        )

    def put(head):
        return pltpu.make_async_copy(
            ob.at[head % OUT_SLOTS, leaf(core)],
            out.at[:, columns(core, head)],
            put_sem.at[head % OUT_SLOTS],
        )

    def give(head):
        return pltpu.make_async_remote_copy(
            src_ref=ob.at[head % OUT_SLOTS, leaf(1 - core)],
            dst_ref=out.at[:, columns(core, head)],
            send_sem=give_sem.at[head % OUT_SLOTS],
            recv_sem=take_sem.at[head],
            device_id=partners[0],
            device_id_type=MESH,
        )

    def take(head):
        return pltpu.make_async_remote_copy(
            src_ref=ob.at[head % OUT_SLOTS, leaf(1 - core)],
            dst_ref=out.at[:, columns(1 - core, head)],
            send_sem=give_sem.at[head % OUT_SLOTS],
            recv_sem=take_sem.at[head],
            device_id=partners[0],
            device_id_type=MESH,
        )

    def matrix(level, i, which):
        at = which
        if not (isinstance(level, int) and level == 0):
            at = lax.rem(which + sides(level), 2)
        return pltpu.make_async_copy(
            (merge_k, merge_v)[i].at[level, :, pl.ds(pl.multiple_of(at * rows, rows), rows)],
            stage.at[2 * level + i, :, pl.ds(which * rows, rows)],
            mat_sem.at[level, i, which],
        )

    gain_levels = [n for n, level in enumerate(levels) if level[0] == "heads"]

    def swap_gain(n, sender):
        span = 2**n
        start = sender // span * span
        return pltpu.make_async_remote_copy(
            src_ref=gb.at[pl.ds(start, span)],
            dst_ref=gb.at[pl.ds(start, span)],
            send_sem=gain_send.at[n],
            recv_sem=gain_recv.at[n],
            device_id=partners[n],
            device_id_type=MESH,
        )

    def gain_step(n):
        if n > 0:
            swap_gain(n - 1, mine).wait_send()
            swap_gain(n - 1, partners[n - 1]["heads"]).wait_recv()
        if n < len(gain_levels):
            swap_gain(n, mine).start()

    own_gain = pltpu.make_async_copy(gain, gb.at[mine], gain_sem)
    own_gain.start()
    def bring(level):
        for i in range(2):
            for which in range(2):
                matrix(level, i, which).start()

    bring(0)
    barrier = pltpu.get_barrier_semaphore()
    for other in partners:
        pl.semaphore_signal(barrier, inc=1, device_id=other, device_id_type=MESH)
    pl.semaphore_wait(barrier, len(partners))

    def fetch(i, head):
        lend(i, head).start()
        load(i, head).start()

    for head in range(min(AHEAD, count)):
        fetch(0, head)
        fetch(1, head)
        if head == 0:
            for level in range(1, merges):
                bring(level)
    own_gain.wait()

    def unpack(level):
        for i in range(2):
            for which in range(2):
                matrix(level, i, which).wait()
            hi, lo = split(stage[2 * level + i])
            mw[level, i, :rows] = hi
            mw[level, i, rows:] = lo

    unpack(0)

    def ready(level, i, head):
        if level == 0:
            load(i, head).wait()
            borrow(i, head).wait_recv()
        else:
            pass_on(level - 1, i, head).wait_recv()

        @pl.when(head >= SLOTS)
        def _():
            pass_on(level, i, head - SLOTS).wait_send()

    def merge(level, i, head):
        if level == 0:
            first, second = xb[i, head, :rows], xb[i, head, rows:]
        else:
            first, second = sb[level - 1, i, head % SLOTS], rb[level - 1, i, head]
        pair = jnp.concatenate([halves(first), halves(second)], axis=0)
        both = dot(mw[level, i], pair)
        summed = both[:rows] + both[rows:]
        sb[level, i, head % SLOTS] = summed[:, :width] + summed[:, width:]

    def when(level, i):
        return STEP * level + i * BEHIND

    def nodes(t, third):
        return [
            (level, i, t - (when(level, i) - third) // 3)
            for i in range(2)
            for level in reversed(range(merges))
            if (when(level, i) - third) % 3 == 0
        ]

    def advance(t, third, guarded):
        todo = nodes(t, third)
        if guarded:

            def send(level, i, head):
                @pl.when((head >= 0) & (head < count))
                def _():
                    pass_on(level, i, head).start()

            earlier = None
            for level, i, head in reversed(todo):

                @pl.when((head >= 0) & (head < count))
                def _(level=level, i=i, head=head):
                    ready(level, i, head)
                    merge(level, i, head)

                if earlier is not None:
                    send(*earlier)
                earlier = (level, i, head)
            if earlier is not None:
                send(*earlier)
        else:
            size = -(-len(todo) // GROUPS) if todo else 1
            for at in range(max(0, (len(todo) - 1) // size * size), -1, -size):
                group = todo[at : at + size]
                for node in group:
                    ready(*node)
                for node in group:
                    merge(*node)
                for node in group:
                    pass_on(*node).start()

    blocks = merges + 2
    spans = blocks * rows // stage.shape[2]

    def gather(cat, i, head, n):
        block = xb[i, head, n * rows : (n + 1) * rows] if n < 2 else rb[n - 2, i, head]
        cat[n * rows : (n + 1) * rows] = halves(block)

    def gathers(cat, i, head):
        return [functools.partial(gather, cat, i, head, n) for n in range(blocks)]

    def score(head, part):
        each = stage.shape[2]
        span = slice(part * rows, (part + 1) * rows)
        query = halves(qb[head, span] * (math.log2(math.e) / math.sqrt(width)))
        query = jnp.concatenate([query, query], axis=1)
        hi, lo = kc[:, :width], kc[:, width:]
        block = dot_nt(query, jnp.concatenate([hi, hi, lo, lo], axis=1))
        for n in range(spans):
            stage[part * spans + n] = block[:, n * each : (n + 1) * each]

    def soften(part, row):
        scores = jnp.concatenate(
            [stage[part * spans + n, row : row + CHUNK] for n in range(spans)], axis=1
        )
        top = jnp.max(scores, axis=1, keepdims=True)
        weights = jnp.exp2(scores - top)
        hi, lo = split(weights)
        at = part * rows + row
        tb[at : at + CHUNK] = jnp.sum(weights, axis=1, keepdims=True)
        wb[at : at + CHUNK] = hi
        wb[2 * rows + at : 2 * rows + at + CHUNK] = lo

    def softens(part):
        return [functools.partial(soften, part, row) for row in range(0, rows, CHUNK)]

    def collect(head):
        for i in range(3):
            lend(i, head).wait_send()

        @pl.when(head >= OUT_SLOTS)
        def _():
            put(head - OUT_SLOTS).wait()
            give(head - OUT_SLOTS).wait_send()

        for part in range(2):
            span = slice(part * rows, (part + 1) * rows)
            low = slice((part + 2) * rows, (part + 3) * rows)
            both = dot(wb[span], vc[...]) + dot(wb[low], vc[...])
            context = (both[:, :width] + both[:, width:]) / tb[span]
            mean_square = jnp.mean(context * context, axis=1, keepdims=True)
            normed = context * lax.rsqrt(mean_square + 1e-06)
            ob[head % OUT_SLOTS, span] = normed * gb[core * count + head]

    lag = -(-max(when(merges - 1, 0) + 3, when(merges - 1, 1) + 1) // 3)

    def request(t):
        @pl.when(t + AHEAD < count)
        def _():
            fetch(0, t + AHEAD)
            fetch(1, t + AHEAD)

        @pl.when((t >= lag - 2) & (t - lag + 2 < count))
        def _():
            fetch(2, t - lag + 2)

    @pl.loop(0, lag)
    def _(t):
        request(t)
        for third in range(3):
            if third < 2:
                for n in range(len(gain_levels) + 1):
                    if n % 2 == third:

                        @pl.when(t == n // 2)
                        def _(n=n):
                            gain_step(n)

            advance(t, third, True)
            for level in range(1, merges):
                before = when(level, 0) - 2
                if before % 3 == third:

                    @pl.when(t == before // 3)
                    def _(level=level):
                        unpack(level)

    def whole(t, guarded):
        head = t - lag
        request(t)
        advance(t, 0, guarded)
        pass_on(merges - 1, 0, head).wait_recv()
        load(2, head).wait()
        borrow(2, head).wait_recv()
        for task in gathers(kc, 0, head):
            task()
        score(head, 0)
        advance(t, 1, guarded)
        score(head, 1)
        for task in softens(0):
            task()
        advance(t, 2, guarded)
        pass_on(merges - 1, 1, head).wait_recv()
        for task in gathers(vc, 1, head) + softens(1):
            task()
        collect(head)
        put(head).start()
        give(head).start()

    @pl.loop(lag, count)
    def _(t):
        whole(t, False)

    @pl.loop(max(lag, count), count + lag)
    def _(t):
        whole(t, True)

    for head in range(count - SLOTS, count):
        for level in range(merges):
            for i in range(2):
                pass_on(level, i, head).wait_send()
    for head in range(count - OUT_SLOTS, count):
        put(head).wait()
        give(head).wait_send()

    @pl.loop(0, count)
    def _(head):
        take(head).wait_recv()


def solution(mesh):
    levels = tree_levels(mesh.shape["ctx"], mesh.shape["heads"])
    merges = len(levels) - 1

    def shards(queries, keys, values, merge_keys, merge_values, out_gain):
        rows, columns = queries.shape
        width = out_gain.shape[1]
        heads = columns // width
        count = heads // 2
        gain_steps = sum(level[0] == "heads" for level in levels)
        dma = pltpu.SemaphoreType.DMA
        return pl.pallas_call(
            functools.partial(kernel, levels),
            out_shape=jax.ShapeDtypeStruct((rows, columns), F32),
            in_specs=[pl.BlockSpec(memory_space=pl.ANY)] * 6,
            out_specs=pl.BlockSpec(memory_space=pl.ANY),
            scratch_shapes=[
                pltpu.VMEM((count, 2 * rows, width), F32),
                pltpu.VMEM((2, count, 2 * rows, width), F32),
                pltpu.VMEM((merges, 2, count, rows, width), F32),
                pltpu.VMEM((merges, 2, SLOTS, rows, width), F32),
                pltpu.VMEM((merges, 2, 2 * rows, 2 * rows), BF16),
                pltpu.VMEM((2 * merges, rows, 2 * rows), F32),
                pltpu.VMEM(((merges + 2) * rows, 2 * width), BF16),
                pltpu.VMEM(((merges + 2) * rows, 2 * width), BF16),
                pltpu.VMEM((4 * rows, (merges + 2) * rows), BF16),
                pltpu.VMEM((2 * rows, 1), F32),
                pltpu.VMEM((OUT_SLOTS, 2 * rows, width), F32),
                pltpu.VMEM((heads, 1, width), F32),
                dma((3, count)),
                dma((3, count)),
                dma((3, count)),
                dma((merges, 2, SLOTS)),
                dma((merges, 2, count)),
                dma((OUT_SLOTS,)),
                dma((OUT_SLOTS,)),
                dma((count,)),
                dma((merges, 2, 2)),
                dma,
                dma((gain_steps,)),
                dma((gain_steps,)),
            ],
            compiler_params=pltpu.CompilerParams(
                collective_id=0, has_side_effects=True, vmem_limit_bytes=67043328
            ),
            name="multipole",
        )(queries, keys, values, merge_keys, merge_values, out_gain)

    return jax.shard_map(
        shards,
        mesh=mesh,
        in_specs=(
            P(("ctx", "heads"), None),
            P(("ctx", "heads"), None),
            P(("ctx", "heads"), None),
            P(),
            P(),
            P("heads", None),
        ),
        out_specs=P(("ctx", "heads"), None),
        check_vma=False,
    )
```
